32 devices in a mesh: depth: 2 (over core), tile: 16 (over z, y, x).
Axes of the slice: x: 2, y: 2, z: 4, core: 2. Of those that a mesh axis runs over, the one named last changes fastest.
Arguments:
- object_layer_slices: float32 [2, 2048, 2, 2048], P('depth', 'tile'), may hold values from 0.2 to 1
- probe_wave: bfloat16 [256, 2, 256], replicated, may hold values from -5 to 5
- propagator: bfloat16 [256, 2, 256], replicated, may hold values from -0.25 to 0.25
- positions: int32 [16, 2, 5, 2], P('tile'), may hold values from 0 to 1792, as said below
- counts: int32 [16, 2], P('tile'), may hold values from 2 to 5
- measured: float32 [16, 2, 5, 256, 256], P('tile'), may hold values from 0 to 2
Outputs:
- object_gradient: float32 [2, 2048, 2, 2048], P('depth', 'tile')
The draws below stay inside these ranges and needn't reach their ends.
Inputs may be any that keep to these rules, and one draw needn't show every extreme that they name: Every window lies inside the object: on tile 0 the first component is 128 or more, on the last tile it is 0 or less; elsewhere it is at most 128, and the second component at most 1792. Slots at or beyond counts[t, b] also hold valid positions. Slots j < counts[t, b] of tile t and micro-batch b are live.
All inputs are finite; a program needn't handle non-finite values.
Results may differ from the reference program's by a relative error of at most 0.013.
Values may be sent and summed in bfloat16 or wider, within the bound.
A program may use at most 192 MiB of HBM per device.

```python
import math
import jax
import jax.numpy as jnp
from jax import lax

P_SIZE = 256
M = 128
TW = 128
LW = 2048
MB = 2
CAP = 5
NS = 2
TILES = 16
NX = 2048
N_TILE = 16


def draw_positions(key, part):
    row_key, column_key = jax.random.split(jax.random.fold_in(key, 11))
    tile_numbers = jnp.arange(TILES, dtype=jnp.int32)[:, None, None]
    lowest = jnp.where(tile_numbers == 0, M, 0).astype(jnp.int32)
    highest = jnp.where(tile_numbers == TILES - 1, TW + M - P_SIZE, TW + 2 * M - P_SIZE).astype(jnp.int32)
    grid_shape = (TILES, MB, CAP)
    lowest = jnp.broadcast_to(lowest, grid_shape)
    highest = jnp.broadcast_to(highest, grid_shape)
    row_begin_points = jax.random.randint(row_key, grid_shape, lowest, highest + 1, dtype=jnp.int32)
    columns = jax.random.randint(column_key, grid_shape, 0, LW - P_SIZE + 1, dtype=jnp.int32)
    return jnp.stack([row_begin_points, columns], axis=-1)


def place_ends(array, key, low, high):
    longest = array.shape.index(max(array.shape))
    spots = []
    for shift in (0, 1):
        where = [jax.random.randint(jax.random.fold_in(key, axis), (), 0, length) for axis, length in enumerate(array.shape)]
        where[longest] = (where[longest] + shift) % array.shape[longest]
        spots.append(tuple(where))
    return array.at[spots[0]].set(low).at[spots[1]].set(high)


def block_scale(rng, shape, pieces, least, top_value):
    level, own = 1.0, jax.random.fold_in(rng, 6)
    for axis_at, shards_of in pieces:
        steps = jnp.exp(jax.random.uniform(jax.random.fold_in(own, axis_at), (shards_of,), jnp.float32, least / len(pieces), top_value / len(pieces)))
        level = level * jnp.repeat(steps, shape[axis_at] // shards_of).reshape([-1 if axis == axis_at else 1 for axis in range(len(shape))])
    return level


def noise(own_key, extent, deviation, limit, kind=jnp.bfloat16):
    values = jax.random.normal(own_key, extent, jnp.float32) * deviation
    return jnp.minimum(jnp.maximum(values, -limit), limit).astype(kind)


def setup_inputs(seed: int = 0) -> dict:
    key_list = jax.random.split(jax.random.key(seed), 7)
    object_layer_slices = jnp.clip(0.2 + 0.8 * jax.random.uniform(key_list[0], (NS, NX, 2, LW), jnp.float32) ** block_scale(key_list[0], (NS, NX, 2, LW), ((0, 2), (1, 16)), -0.2, 0.2), 0.2, 1.0)
    probe_wave = noise(key_list[1], (P_SIZE, 2, P_SIZE), 0.7, 5.0)
    propagator = noise(key_list[2], (P_SIZE, 2, P_SIZE), (2 * P_SIZE) ** -0.5, 0.25)
    positions = draw_positions(jax.random.fold_in(key_list[6], 71), 0)
    counts = place_ends(jax.random.randint(key_list[4], (TILES, MB), 2, CAP + 1), jax.random.fold_in(key_list[4], 1), 2, CAP).astype(jnp.int32)
    measured = jnp.clip(2.0 * jax.random.uniform(key_list[5], (TILES, MB, CAP, P_SIZE, P_SIZE), jnp.float32) ** block_scale(key_list[5], (TILES, MB, CAP, P_SIZE, P_SIZE), ((0, 16),), -0.2, 0.2), 0.0, 2.0)
    return dict(object_layer_slices=object_layer_slices, probe_wave=probe_wave, propagator=propagator, positions=positions, counts=counts, measured=measured)


def dft_table(side_cells):
    index_of_row = jnp.arange(side_cells, dtype=jnp.int32)
    phases = index_of_row[:, None] * index_of_row[None, :] % side_cells
    angles = phases.astype(jnp.float32) * (2.0 * math.pi / side_cells)
    factor = 1.0 / math.sqrt(side_cells)
    return jnp.stack([jnp.cos(angles) * factor, -jnp.sin(angles) * factor], axis=1).astype(jnp.bfloat16)

def conj_transpose(matrix):
    flipped = jnp.transpose(matrix, (2, 1, 0))
    return jnp.stack([flipped[:, 0], -flipped[:, 1]], axis=1)

def block_pair(matrix):
    real_part = matrix[:, 0]
    imag_part = matrix[:, 1]
    side_cells = real_part.shape[0]
    upper_half = jnp.stack([real_part, -imag_part], axis=2)
    lower_half = jnp.stack([imag_part, real_part], axis=2)
    leftward_block = jnp.stack([upper_half, lower_half], axis=1)
    right_block = jnp.transpose(leftward_block, (3, 2, 1, 0)).reshape(2 * side_cells, 2 * side_cells)
    return (leftward_block.reshape(2 * side_cells, 2 * side_cells), right_block)

def transform(blocks, wave_in):
    leftward_block, right_block = blocks
    slot_count, side_cells = (wave_in.shape[0], wave_in.shape[1])
    stacked_arrays = wave_in.reshape(slot_count, 2 * side_cells, side_cells).astype(jnp.float32)
    central_part = jnp.einsum('rj,tjg->trg', leftward_block.astype(jnp.float32), stacked_arrays, precision=lax.Precision.HIGHEST)
    central_part = central_part.astype(jnp.bfloat16).reshape(slot_count, side_cells, 2 * side_cells).astype(jnp.float32)
    result = jnp.einsum('cib,bk->cik', central_part, right_block.astype(jnp.float32), precision=lax.Precision.HIGHEST)
    return result.reshape(slot_count, side_cells, 2, side_cells)

def complex_product(first_wave, second_wave, conjugate):
    first_real = first_wave[..., 0, :].astype(jnp.float32)
    first_imag = first_wave[..., 1, :].astype(jnp.float32)
    second_real = second_wave[..., 0, :].astype(jnp.float32)
    second_imag = second_wave[..., 1, :].astype(jnp.float32)
    if conjugate:
        first_imag = -first_imag
    return jnp.stack([first_real * second_real - first_imag * second_imag, first_real * second_imag + first_imag * second_real], axis=-2)

def cut_windows(extended, placements):

    def single(placement):
        anchor = jnp.zeros((), jnp.int32)
        return lax.dynamic_slice(extended, (anchor, placement[0].astype(jnp.int32), anchor, placement[1].astype(jnp.int32)), (extended.shape[0], P_SIZE, 2, P_SIZE))
    return jax.vmap(single)(placements)

def add_patches(totals, patches, placements):
    for slot_no in range(patches.shape[0]):
        anchor = jnp.zeros((), jnp.int32)
        corner = (anchor, placements[slot_no, 0].astype(jnp.int32), anchor, placements[slot_no, 1].astype(jnp.int32))
        current = lax.dynamic_slice(totals, corner, patches.shape[1:])
        totals = lax.dynamic_update_slice(totals, current + patches[slot_no], corner)
    return totals

def forward_section(windows, wave_in, forward_list):
    entering = []
    leaving = None
    for slice_no in range(len(forward_list)):
        entering.append(wave_in)
        product = complex_product(windows[:, slice_no], wave_in, False).astype(jnp.bfloat16)
        leaving = transform(forward_list[slice_no], product)
        wave_in = leaving.astype(jnp.bfloat16)
    return (jnp.stack(entering, axis=0), leaving)

def backward_section(windows, entering, incoming, backward_list):
    patches = []
    for slice_no in reversed(range(len(backward_list))):
        spread = transform(backward_list[slice_no], incoming.astype(jnp.bfloat16)).astype(jnp.bfloat16)
        patches.insert(0, complex_product(entering[slice_no], spread, True))
        incoming = complex_product(windows[:, slice_no], spread, True)
    return jnp.stack(patches, axis=1)

def far_gradient(far_field, observed, live_slots):
    real_part = far_field[:, :, 0, :]
    imag_part = far_field[:, :, 1, :]
    weight = live_slots.astype(jnp.float32)[:, None, None]
    misfit = weight * (real_part * real_part + imag_part * imag_part - observed)
    return jnp.stack([misfit * real_part, misfit * imag_part], axis=2)

def reference(object_layer_slices, probe_wave, propagator, positions, counts, measured):
    all_slices = object_layer_slices.shape[0]
    detector = dft_table(P_SIZE)
    forward_list = [block_pair(propagator)] * (all_slices - 1) + [block_pair(detector)]
    backward_list = [block_pair(conj_transpose(propagator))] * (all_slices - 1) + [block_pair(conj_transpose(detector))]
    padded = jnp.pad(object_layer_slices, ((0, 0), (M, M), (0, 0), (0, 0)))
    start_wave = jnp.broadcast_to(probe_wave, (CAP, P_SIZE, 2, P_SIZE))

    def per_tile(totals, inputs):
        tile_no, tile_places, tile_counts, tile_measured = inputs
        first_row = (tile_no * TW).astype(jnp.int32)
        extended = lax.dynamic_slice_in_dim(padded, first_row, TW + 2 * M, 1)
        tile_sums = jnp.zeros(extended.shape, jnp.float32)
        for batch_no in range(MB):
            placements = tile_places[batch_no]
            live_slots = jnp.arange(CAP, dtype=jnp.int32) < tile_counts[batch_no]
            windows = cut_windows(extended, placements)
            entering, far_field = forward_section(windows, start_wave, forward_list)
            incoming = far_gradient(far_field, tile_measured[batch_no], live_slots)
            patches = backward_section(windows, entering, incoming, backward_list)
            tile_sums = add_patches(tile_sums, patches, placements)
        current = lax.dynamic_slice_in_dim(totals, first_row, TW + 2 * M, 1)
        totals = lax.dynamic_update_slice_in_dim(totals, current + tile_sums, first_row, 1)
        return (totals, None)
    totals = jnp.zeros(padded.shape, jnp.float32)
    tile_numbers = jnp.arange(N_TILE, dtype=jnp.int32)
    totals, ignored = lax.scan(per_tile, totals, (tile_numbers, positions, counts, measured))
    return totals[:, M:M + N_TILE * TW]
```

```python
import functools
import math

import jax
import jax.numpy as jnp
import numpy as np
from jax import lax
from jax.experimental import pallas as pl
from jax.experimental.pallas import tpu as pltpu
from jax.sharding import PartitionSpec as P

LANES = 128
CHUNKS = 4


VMEM = pl.BlockSpec(memory_space=pltpu.VMEM)
SMEM = pl.BlockSpec(memory_space=pltpu.SMEM)


def dft_block(side):
    index = np.arange(side)
    angles = (index[:, None] * index[None, :] % side) * (2.0 * math.pi / side)
    factor = 1.0 / math.sqrt(side)
    real, imag = np.cos(angles) * factor, -np.sin(angles) * factor
    return np.block([[real, -imag], [imag, real]]).astype(np.float32).astype(jnp.bfloat16)


def complex_block(matrix):
    real, imag = matrix[:, 0], matrix[:, 1]
    return jnp.concatenate(
        [jnp.concatenate([real, -imag], axis=1), jnp.concatenate([imag, real], axis=1)], axis=0
    )


def spot(pos_ref, slot, blocks, wide):
    row, column = pos_ref[slot, 0], pos_ref[slot, 1]
    block = jnp.minimum(column // LANES, blocks - wide - 1)
    return row, block, column - block * LANES


def cut_kernel(tile_rows, pos_ref, off_ref, mid_refs, near_refs, far_refs, keep_ref, send_ref, ext):
    margin = near_refs[0].shape[2]
    base = 0
    for mid, near, far in zip(mid_refs, near_refs, far_refs):
        span = pl.ds(base, mid.shape[0])
        ext[span, :, pl.ds(margin, tile_rows), :] = mid[...].astype(jnp.float32)
        ext[span, :, pl.ds(pl.multiple_of(off_ref[0], 8), margin), :] = near[...].astype(jnp.float32)
        ext[span, :, pl.ds(pl.multiple_of(off_ref[1], 8), margin), :] = far[...].astype(jnp.float32)
        base += mid.shape[0]
    slots, side = keep_ref.shape[0], keep_ref.shape[2]
    wide = side // LANES
    lane = lax.broadcasted_iota(jnp.int32, (side, LANES), 1)

    def cut(out_ref, first):
        def body(slot, carry):
            row, block, shift = spot(pos_ref, slot + first, ext.shape[0], wide)
            turn = lax.rem(LANES - shift, LANES)
            inside = lane < LANES - shift
            for part in range(2):
                pieces = [
                    pltpu.roll(ext[block + k, part, pl.ds(row, side), :], turn, axis=1)
                    for k in range(wide + 1)
                ]
                for k in range(wide):
                    out_ref[slot, part, :, k * LANES : (k + 1) * LANES] = jnp.where(
                        inside, pieces[k], pieces[k + 1]
                    ).astype(jnp.bfloat16)
            return carry

        lax.fori_loop(0, slots, body, 0)

    cut(keep_ref, 0)
    cut(send_ref, slots)


def wave_kernel(
    info_ref, keep_ref, recv_ref, meas_ref, probe_ref, prop_ref, prop_t_ref, dft_ref, dft_t_ref,
    mine_ref, other_ref,
):
    f32, bf16 = jnp.float32, jnp.bfloat16
    first = info_ref[0] == 0
    live = (pl.program_id(0) < info_ref[1]).astype(f32)
    side = probe_ref.shape[1]

    def field(part):
        mine, other = keep_ref[0, part], recv_ref[0, part]
        return (
            jnp.where(first, mine, other).astype(f32),
            jnp.where(first, other, mine).astype(f32),
        )

    def transform(left, right, real, imag):
        stacked = jnp.concatenate([real.astype(bf16), imag.astype(bf16)], axis=0)
        half = jnp.dot(left[...], stacked, preferred_element_type=f32).astype(bf16)
        across = jnp.concatenate([half[:side], half[side:]], axis=1)
        whole = jnp.dot(across, right[...], preferred_element_type=f32)
        return whole[:, :side], whole[:, side:]

    def rounded(pair):
        return tuple(value.astype(bf16).astype(f32) for value in pair)

    def times(a, b):
        return a[0] * b[0] - a[1] * b[1], a[0] * b[1] + a[1] * b[0]

    def conj_times(a, b):
        return a[0] * b[0] + a[1] * b[1], a[0] * b[1] - a[1] * b[0]

    (x0r, x1r), (x0i, x1i) = field(0), field(1)
    x0, x1 = (x0r, x0i), (x1r, x1i)
    psi0 = (probe_ref[0].astype(f32), probe_ref[1].astype(f32))
    psi1 = rounded(transform(prop_ref, prop_t_ref, *times(psi0, x0)))
    far = transform(dft_ref, dft_t_ref, *times(psi1, x1))
    misfit = live * (far[0] * far[0] + far[1] * far[1] - meas_ref[0, 0, 0])
    g1 = rounded(transform(dft_t_ref, dft_ref, misfit * far[0], misfit * far[1]))
    patch1 = conj_times(psi1, g1)
    g0 = rounded(transform(prop_t_ref, prop_ref, *conj_times(x1, g1)))
    patch0 = conj_times(psi0, g0)
    for part in range(2):
        a, b = patch0[part].astype(bf16), patch1[part].astype(bf16)
        mine_ref[0, part] = jnp.where(first, a, b)
        other_ref[0, part] = jnp.where(first, b, a)


def add_kernel(pos_ref, off_ref, mine_ref, recv_ref, inner_ref, near_refs, far_refs, total):
    total[...] = jnp.zeros_like(total)
    slots, side = mine_ref.shape[0], mine_ref.shape[2]
    wide = side // LANES
    lane = lax.broadcasted_iota(jnp.int32, (side, LANES), 1)

    def add(patch_ref, first):
        def body(slot, carry):
            row, block, shift = spot(pos_ref, slot + first, total.shape[0], wide)
            turn = lax.rem(shift, LANES)
            inside = lane >= shift
            for part in range(2):
                pieces = [
                    pltpu.roll(
                        patch_ref[slot, part, :, k * LANES : (k + 1) * LANES].astype(jnp.float32),
                        turn,
                        axis=1,
                    )
                    for k in range(wide)
                ]
                pieces = [jnp.zeros_like(pieces[0])] + pieces + [jnp.zeros_like(pieces[0])]
                for k in range(wide + 1):
                    total[block + k, part, pl.ds(row, side), :] += jnp.where(
                        inside, pieces[k + 1], pieces[k]
                    )
            return carry

        lax.fori_loop(0, slots, body, 0)

    add(mine_ref, 0)
    add(recv_ref, slots)
    margin, rows = near_refs[0].shape[2], inner_ref.shape[2]
    inner_ref[...] = total[:, :, pl.ds(margin, rows), :]
    base = 0
    for near, far in zip(near_refs, far_refs):
        span = pl.ds(base, near.shape[0])
        near[...] = total[span, :, pl.ds(pl.multiple_of(off_ref[0], 8), margin), :].astype(
            jnp.bfloat16
        )
        far[...] = total[span, :, pl.ds(pl.multiple_of(off_ref[1], 8), margin), :].astype(
            jnp.bfloat16
        )
        base += near.shape[0]


def local(object_layer_slices, probe_wave, propagator, positions, counts, measured):
    f32, bf16 = jnp.float32, jnp.bfloat16
    section, tile = lax.axis_index("depth"), lax.axis_index("tile")
    sections, tiles = lax.axis_size("depth"), lax.axis_size("tile")
    side = probe_wave.shape[0]
    _, rows, _, columns = object_layer_slices.shape
    slots = positions.shape[2]
    margin = side // 2
    assert sections == 2 and positions.shape[1] == sections and object_layer_slices.shape[0] == 1
    assert tiles % 2 == 0 and rows == margin
    blocks = columns // LANES
    per = blocks // CHUNKS
    even = tile % 2 == 0

    swap_tile = [(t, t ^ 1) for t in range(tiles)]
    swap_core = [(0, 1), (1, 0)]
    spread = [(t, t + 2 - 4 * (t % 2)) for t in range(tiles)]
    spread = [(a, b) for a, b in spread if 0 <= b < tiles]
    gather = [(b, a) for a, b in spread]

    mine = [
        object_layer_slices[0, :, :, q * per * LANES : (q + 1) * per * LANES]
        .astype(bf16)
        .reshape(rows, 2, per, LANES)
        .transpose(2, 1, 0, 3)
        for q in range(CHUNKS)
    ]
    near = [lax.ppermute(m, "tile", swap_tile) for m in mine]
    far = [lax.ppermute(m, "tile", spread) for m in near]

    partner = 1 - section
    pos = jnp.concatenate(
        [
            lax.dynamic_index_in_dim(positions[0], section, 0, False),
            lax.dynamic_index_in_dim(positions[0], partner, 0, False),
        ],
        axis=0,
    )
    offsets = jnp.where(even, jnp.array([margin + rows, 0]), jnp.array([0, margin + rows]))
    offsets = offsets.astype(jnp.int32)
    extent = (blocks, 2, rows + 2 * margin, LANES)
    window = jax.ShapeDtypeStruct((slots, 2, side, side), bf16)

    keep, send = pl.pallas_call(
        functools.partial(cut_kernel, rows),
        out_shape=(window, window),
        in_specs=[SMEM, SMEM, [VMEM] * CHUNKS, [VMEM] * CHUNKS, [VMEM] * CHUNKS],
        out_specs=(VMEM, VMEM),
        scratch_shapes=[pltpu.VMEM(extent, f32)],
        name="cut",
    )(pos, offsets, mine, near, far)
    recv = lax.ppermute(send, "depth", swap_core)

    prop = complex_block(propagator)
    dft = dft_block(side)
    info = jnp.stack(
        [section, lax.dynamic_index_in_dim(counts[0], section, 0, False)]
    ).astype(jnp.int32)
    window_spec = pl.BlockSpec((1, 2, side, side), lambda i, info: (i, 0, 0, 0))
    matrix_spec = pl.BlockSpec((2 * side, 2 * side), lambda i, info: (0, 0))
    patch_mine, patch_other = pl.pallas_call(
        wave_kernel,
        out_shape=(window, window),
        grid_spec=pltpu.PrefetchScalarGridSpec(
            num_scalar_prefetch=1,
            grid=(slots,),
            in_specs=[
                window_spec,
                window_spec,
                pl.BlockSpec((1, 1, 1, side, side), lambda i, info: (0, info[0], i, 0, 0)),
                pl.BlockSpec((2, side, side), lambda i, info: (0, 0, 0)),
            ]
            + [matrix_spec] * 4,
            out_specs=(window_spec, window_spec),
        ),
        name="wave",
    )(
        info, keep, recv, measured, probe_wave.transpose(1, 0, 2),
        prop, prop.T, jnp.asarray(dft), jnp.asarray(np.ascontiguousarray(dft.T)),
    )
    patch_recv = lax.ppermute(patch_other, "depth", swap_core)

    rim = jax.ShapeDtypeStruct((per, 2, margin, LANES), bf16)
    inner, near_out, far_out = pl.pallas_call(
        add_kernel,
        out_shape=(
            jax.ShapeDtypeStruct((blocks, 2, rows, LANES), f32), [rim] * CHUNKS, [rim] * CHUNKS
        ),
        in_specs=[SMEM, SMEM, VMEM, VMEM],
        out_specs=(VMEM, [VMEM] * CHUNKS, [VMEM] * CHUNKS),
        scratch_shapes=[pltpu.VMEM(extent, f32)],
        name="add",
    )(pos, offsets, patch_mine, patch_recv)
    passed = [lax.ppermute(m, "tile", gather) for m in far_out]
    joined = [(a.astype(f32) + b.astype(f32)).astype(bf16) for a, b in zip(near_out, passed)]
    arrived = [lax.ppermute(m, "tile", swap_tile) for m in joined]
    result = [
        (inner[q * per : (q + 1) * per] + arrived[q].astype(f32))
        .transpose(2, 1, 0, 3)
        .reshape(rows, 2, per * LANES)
        for q in range(CHUNKS)
    ]
    return jnp.concatenate(result, axis=2)[None]


def solution(mesh):
    placed = (
        P("depth", "tile", None, None),
        P(),
        P(),
        P("tile", None, None, None),
        P("tile", None),
        P("tile", None, None, None, None),
    )
    return jax.shard_map(
        local, mesh=mesh, in_specs=placed, out_specs=P("depth", "tile", None, None), check_vma=False
    )
```

```python
import math

import jax
import jax.numpy as jnp
import numpy as np
from jax import lax
from jax.experimental import pallas as pl
from jax.experimental.pallas import tpu as pltpu
from jax.sharding import PartitionSpec as P

LANES = 128
CHUNKS = 8
MESH = pl.DeviceIdType.MESH
VMEM = pl.BlockSpec(memory_space=pltpu.VMEM)
SMEM = pl.BlockSpec(memory_space=pltpu.SMEM)
ANY = pl.BlockSpec(memory_space=pl.ANY)
f32, bf16 = jnp.float32, jnp.bfloat16


def dft_block(side):
    index = np.arange(side)
    angles = (index[:, None] * index[None, :] % side) * (2.0 * math.pi / side)
    factor = 1.0 / math.sqrt(side)
    real, imag = np.cos(angles) * factor, -np.sin(angles) * factor
    return np.block([[real, -imag], [imag, real]]).astype(np.float32).astype(bf16)


def route():
    tile, tiles = lax.axis_index("tile"), lax.axis_size("tile")
    odd = lax.rem(tile, 2)
    outward = tile + 2 - 4 * odd
    inward = tile - 2 + 4 * odd
    sends = (outward >= 0) & (outward < tiles)
    takes = (inward >= 0) & (inward < tiles)
    return odd, tile + 1 - 2 * odd, outward, inward, sends, takes


def greet(cores):
    odd, partner, outward, inward, sends, takes = route()
    barrier = pltpu.get_barrier_semaphore()
    pl.semaphore_signal(barrier, inc=1, device_id={"tile": partner}, device_id_type=MESH)
    expected = 1 + sends.astype(jnp.int32) + takes.astype(jnp.int32)
    if cores:
        other = 1 - lax.axis_index("depth")
        pl.semaphore_signal(barrier, inc=1, device_id={"depth": other}, device_id_type=MESH)
        expected = expected + 1

    @pl.when(sends)
    def _():
        pl.semaphore_signal(barrier, inc=1, device_id={"tile": outward}, device_id_type=MESH)

    @pl.when(takes)
    def _():
        pl.semaphore_signal(barrier, inc=1, device_id={"tile": inward}, device_id_type=MESH)

    pl.semaphore_wait(barrier, expected)


def remote(src, dst, sems, slot, target):
    return pltpu.make_async_remote_copy(
        src_ref=src, dst_ref=dst, send_sem=sems.at[0, slot], recv_sem=sems.at[1, slot],
        device_id=target, device_id_type=MESH,
    )


def spot(pos_ref, batch, slot, blocks, wide):
    row, column = pos_ref[0, batch, slot, 0], pos_ref[0, batch, slot, 1]
    block = jnp.minimum(lax.shift_right_logical(column, 7), blocks - wide - 1)
    return row, block, column - block * LANES


def main_kernel(
    pos_ref, count_ref, mine_ref, meas_ref, probe_ref, prop_ref, dft_ref, dft_t_ref,
    own_ref, recv_ref,
    near, far, ext, send_win, keep_win, recv_win, other, meas, prop, prop_t,
    near_sem, far_sem, win_sem, patch_sem, meas_sem,
):
    odd, partner, outward, inward, sends, takes = route()
    section = lax.axis_index("depth")
    core = {"depth": 1 - section}
    blocks, _, rows, _ = mine_ref.shape
    margin = near.shape[2]
    per = blocks // CHUNKS
    slots, side = own_ref.shape[0], own_ref.shape[2]
    wide = side // LANES
    greet(True)

    def near_copy(q):
        span = pl.ds(q * per, per)
        return remote(mine_ref.at[span], near.at[span], near_sem, q, {"tile": partner})

    def far_copy(q):
        span = pl.ds(q * per, per)
        return remote(near.at[span], far.at[span], far_sem, q, {"tile": outward})

    def loop(count, body):
        def step(i, carry):
            body(i)
            return carry

        lax.fori_loop(0, count, step, 0)

    loop(CHUNKS, lambda q: near_copy(q).start())
    meas_copy = pltpu.make_async_copy(meas_ref.at[0, section], meas, meas_sem)
    meas_copy.start()

    real, imag = prop_ref[0].astype(f32), prop_ref[1].astype(f32)
    real_t, imag_t = real.T, imag.T
    for ref, re, up, down in ((prop, real, -imag, imag), (prop_t, real_t, imag_t, -imag_t)):
        ref[:side, :side] = re.astype(bf16)
        ref[:side, side:] = up.astype(bf16)
        ref[side:, :side] = down.astype(bf16)
        ref[side:, side:] = re.astype(bf16)

    near_row = pl.multiple_of((1 - odd) * (margin + rows), 8)
    far_row = pl.multiple_of(odd * (margin + rows), 8)

    def fill(q, source, row):
        span = pl.ds(q * per, per)
        ext[span, :, pl.ds(row, source.shape[2]), :] = source[span].astype(f32)

    loop(CHUNKS, lambda q: fill(q, mine_ref, margin))

    def pass_on(q):
        near_copy(q).wait_recv()

        @pl.when(sends)
        def _():
            far_copy(q).start()

        fill(q, near, near_row)

    loop(CHUNKS, pass_on)

    def take(q):
        @pl.when(takes)
        def _():
            far_copy(q).wait_recv()
            fill(q, far, far_row)

        @pl.when(jnp.logical_not(takes))
        def _():
            span = pl.ds(q * per, per)
            ext[span, :, pl.ds(far_row, margin), :] = jnp.zeros((per, 2, margin, LANES), f32)

    loop(CHUNKS, take)

    lane = lax.broadcasted_iota(jnp.int32, (side, LANES), 1)

    def cut(out_ref, batch, slot):
        row, block, shift = spot(pos_ref, batch, slot, blocks, wide)
        turn = lax.rem(LANES - shift, LANES)
        inside = lane < LANES - shift
        for part in range(2):
            pieces = [
                pltpu.roll(ext[block + k, part, pl.ds(row, side), :], turn, axis=1)
                for k in range(wide + 1)
            ]
            for k in range(wide):
                out_ref[slot, part, :, k * LANES : (k + 1) * LANES] = jnp.where(
                    inside, pieces[k], pieces[k + 1]
                ).astype(bf16)

    def window_copy(slot):
        return remote(send_win.at[slot], recv_win.at[slot], win_sem, slot, core)

    def patch_copy(slot):
        return remote(other.at[slot], recv_ref.at[slot], patch_sem, slot, core)

    def cut_send(slot):
        cut(send_win, 1 - section, slot)

        @pl.when(slot > 0)
        def _():
            window_copy(slot - 1).start()

    loop(slots, cut_send)

    def cut_keep(slot):
        cut(keep_win, section, slot)

        @pl.when(slot == 0)
        def _():
            window_copy(slots - 1).start()

    loop(slots, cut_keep)
    meas_copy.wait()

    def transform(left, right, real, imag):
        stacked = jnp.concatenate([real.astype(bf16), imag.astype(bf16)], axis=0)
        half = jnp.dot(left[...], stacked, preferred_element_type=f32).astype(bf16)
        across = jnp.concatenate([half[:side], half[side:]], axis=1)
        whole = jnp.dot(across, right[...], preferred_element_type=f32)
        return whole[:, :side], whole[:, side:]

    def rounded(pair):
        return tuple(value.astype(bf16).astype(f32) for value in pair)

    def times(a, b):
        return a[0] * b[0] - a[1] * b[1], a[0] * b[1] + a[1] * b[0]

    def conj_times(a, b):
        return a[0] * b[0] + a[1] * b[1], a[0] * b[1] - a[1] * b[0]

    def wave(slot):
        window_copy(slot).wait_recv()
        first = section == 0
        live = (slot < count_ref[0, section]).astype(f32)

        def field(part):
            a, b = keep_win[slot, part], recv_win[slot, part]
            return jnp.where(first, a, b).astype(f32), jnp.where(first, b, a).astype(f32)

        (x0r, x1r), (x0i, x1i) = field(0), field(1)
        x0, x1 = (x0r, x0i), (x1r, x1i)
        psi0 = (probe_ref[0].astype(f32), probe_ref[1].astype(f32))
        psi1 = rounded(transform(prop, prop_t, *times(psi0, x0)))
        wave_far = transform(dft_ref, dft_t_ref, *times(psi1, x1))
        misfit = live * (wave_far[0] * wave_far[0] + wave_far[1] * wave_far[1] - meas[slot])
        g1 = rounded(transform(dft_t_ref, dft_ref, misfit * wave_far[0], misfit * wave_far[1]))
        patch1 = conj_times(psi1, g1)
        g0 = rounded(transform(prop_t, prop, *conj_times(x1, g1)))
        patch0 = conj_times(psi0, g0)
        for part in range(2):
            a, b = patch0[part].astype(bf16), patch1[part].astype(bf16)
            own_ref[slot, part] = jnp.where(first, a, b)
            other[slot, part] = jnp.where(first, b, a)

        @pl.when(slot > 0)
        def _():
            patch_copy(slot - 1).start()

    loop(slots, wave)

    def settle(q):
        near_copy(q).wait_send()

        @pl.when(sends)
        def _():
            far_copy(q).wait_send()

    loop(CHUNKS, settle)
    loop(slots, lambda slot: window_copy(slot).wait_send())
    patch_copy(slots - 1).start()
    loop(slots, lambda slot: patch_copy(slot).wait())


def add_kernel(pos_ref, own_ref, recv_ref, inner_ref, near_ref, far_ref, total):
    odd = route()[0]
    section = lax.axis_index("depth")
    total[...] = jnp.zeros_like(total)
    slots, side = own_ref.shape[0], own_ref.shape[2]
    wide = side // LANES
    lane = lax.broadcasted_iota(jnp.int32, (side, LANES), 1)

    def add(patch_ref, batch):
        def body(slot, carry):
            row, block, shift = spot(pos_ref, batch, slot, total.shape[0], wide)
            turn = lax.rem(shift, LANES)
            inside = lane >= shift
            for part in range(2):
                pieces = [
                    pltpu.roll(
                        patch_ref[slot, part, :, k * LANES : (k + 1) * LANES].astype(f32),
                        turn,
                        axis=1,
                    )
                    for k in range(wide)
                ]
                pieces = [jnp.zeros_like(pieces[0])] + pieces + [jnp.zeros_like(pieces[0])]
                for k in range(wide + 1):
                    total[block + k, part, pl.ds(row, side), :] += jnp.where(
                        inside, pieces[k + 1], pieces[k]
                    )
            return carry

        lax.fori_loop(0, slots, body, 0)

    add(own_ref, section)
    add(recv_ref, 1 - section)
    margin, rows = near_ref.shape[2], inner_ref.shape[2]
    near_row = pl.multiple_of((1 - odd) * (margin + rows), 8)
    far_row = pl.multiple_of(odd * (margin + rows), 8)
    inner_ref[...] = total[:, :, pl.ds(margin, rows), :]
    near_ref[...] = total[:, :, pl.ds(near_row, margin), :].astype(bf16)
    far_ref[...] = total[:, :, pl.ds(far_row, margin), :].astype(bf16)


def home_kernel(inner_ref, near_ref, far_ref, out_ref, passed, joined, arrived, far_sem, near_sem):
    odd, partner, outward, inward, sends, takes = route()
    blocks = inner_ref.shape[0]
    per = blocks // CHUNKS
    greet(False)

    def loop(body):
        def step(i, carry):
            body(i)
            return carry

        lax.fori_loop(0, CHUNKS, step, 0)

    def far_copy(q):
        span = pl.ds(q * per, per)
        return remote(far_ref.at[span], passed.at[span], far_sem, q, {"tile": inward})

    def near_copy(q):
        span = pl.ds(q * per, per)
        return remote(joined.at[span], arrived.at[span], near_sem, q, {"tile": partner})

    @pl.when(takes)
    def _():
        loop(lambda q: far_copy(q).start())

    def join(q):
        span = pl.ds(q * per, per)

        @pl.when(sends)
        def _():
            far_copy(q).wait_recv()
            joined[span] = (near_ref[span].astype(f32) + passed[span].astype(f32)).astype(bf16)

        @pl.when(jnp.logical_not(sends))
        def _():
            joined[span] = near_ref[span]

        near_copy(q).start()

    loop(join)

    def finish(q):
        span = pl.ds(q * per, per)
        near_copy(q).wait_recv()
        out_ref[span] = inner_ref[span] + arrived[span].astype(f32)

    loop(finish)

    def settle(q):
        near_copy(q).wait_send()

        @pl.when(takes)
        def _():
            far_copy(q).wait_send()

    loop(settle)


def local(object_layer_slices, probe_wave, propagator, positions, counts, measured):
    side = probe_wave.shape[0]
    _, rows, _, columns = object_layer_slices.shape
    slots = positions.shape[2]
    margin = side // 2
    sections, tiles = lax.axis_size("depth"), lax.axis_size("tile")
    assert sections == 2 and positions.shape[1] == sections and object_layer_slices.shape[0] == 1
    assert tiles % 2 == 0 and rows == margin
    blocks = columns // LANES
    extent = (blocks, 2, rows + 2 * margin, LANES)
    tile_shape, window_shape = (blocks, 2, margin, LANES), (slots, 2, side, side)
    tile_bf16 = jax.ShapeDtypeStruct(tile_shape, bf16)
    tile_f32 = jax.ShapeDtypeStruct(tile_shape, f32)
    window = jax.ShapeDtypeStruct(window_shape, bf16)

    mine = (
        object_layer_slices[0].astype(bf16).reshape(rows, 2, blocks, LANES).transpose(2, 1, 0, 3)
    )
    dft = dft_block(side)
    own, recv = pl.pallas_call(
        main_kernel,
        out_shape=(window, window),
        in_specs=[SMEM, SMEM, VMEM, ANY, VMEM, VMEM, VMEM, VMEM],
        out_specs=(VMEM, VMEM),
        scratch_shapes=[pltpu.VMEM(tile_shape, bf16)] * 2
        + [pltpu.VMEM(extent, f32)]
        + [pltpu.VMEM(window_shape, bf16)] * 4
        + [pltpu.VMEM((slots, side, side), f32)]
        + [pltpu.VMEM((2 * side, 2 * side), bf16)] * 2
        + [pltpu.SemaphoreType.DMA((2, CHUNKS))] * 2
        + [pltpu.SemaphoreType.DMA((2, slots))] * 2
        + [pltpu.SemaphoreType.DMA],
        compiler_params=pltpu.CompilerParams(collective_id=0, has_side_effects=True),
        name="waves",
    )(
        positions, counts, mine, measured, probe_wave.transpose(1, 0, 2),
        propagator.transpose(1, 0, 2), jnp.asarray(dft), jnp.asarray(np.ascontiguousarray(dft.T)),
    )
    inner, near, far = pl.pallas_call(
        add_kernel,
        out_shape=(tile_f32, tile_bf16, tile_bf16),
        in_specs=[SMEM, VMEM, VMEM],
        out_specs=(VMEM, VMEM, VMEM),
        scratch_shapes=[pltpu.VMEM(extent, f32)],
        name="add",
    )(positions, own, recv)
    total = pl.pallas_call(
        home_kernel,
        out_shape=tile_f32,
        in_specs=[VMEM] * 3,
        out_specs=VMEM,
        scratch_shapes=[pltpu.VMEM(tile_shape, bf16)] * 3
        + [pltpu.SemaphoreType.DMA((2, CHUNKS))] * 2,
        compiler_params=pltpu.CompilerParams(collective_id=1, has_side_effects=True),
        name="home",
    )(inner, near, far)
    return total.transpose(2, 1, 0, 3).reshape(1, rows, 2, columns)


def solution(mesh):
    placed = (
        P("depth", "tile", None, None),
        P(),
        P(),
        P("tile", None, None, None),
        P("tile", None),
        P("tile", None, None, None, None),
    )
    return jax.shard_map(
        local, mesh=mesh, in_specs=placed, out_specs=P("depth", "tile", None, None), check_vma=False
    )
```

```python
import math

import jax
import jax.numpy as jnp
import numpy as np
from jax import lax
from jax.experimental import pallas as pl
from jax.experimental.pallas import tpu as pltpu
from jax.sharding import PartitionSpec as P

LANES = 128
CHUNKS = 16
MESH = pl.DeviceIdType.MESH
VMEM = pl.BlockSpec(memory_space=pltpu.VMEM)
SMEM = pl.BlockSpec(memory_space=pltpu.SMEM)
HBM = pl.BlockSpec(memory_space=pltpu.HBM)
f32, bf16 = jnp.float32, jnp.bfloat16


def dft_block(side):
    index = np.arange(side)
    angles = (index[:, None] * index[None, :] % side) * (2.0 * math.pi / side)
    factor = 1.0 / math.sqrt(side)
    real, imag = np.cos(angles) * factor, -np.sin(angles) * factor
    return np.block([[real, -imag], [imag, real]]).astype(np.float32).astype(bf16)


def route():
    tile, tiles = lax.axis_index("tile"), lax.axis_size("tile")
    odd = lax.rem(tile, 2)
    outward = tile + 2 - 4 * odd
    inward = tile - 2 + 4 * odd
    sends = (outward >= 0) & (outward < tiles)
    takes = (inward >= 0) & (inward < tiles)
    return odd, tile + 1 - 2 * odd, outward, inward, sends, takes


def greet(cores):
    odd, partner, outward, inward, sends, takes = route()
    barrier = pltpu.get_barrier_semaphore()
    pl.semaphore_signal(barrier, inc=1, device_id={"tile": partner}, device_id_type=MESH)
    expected = 1 + sends.astype(jnp.int32) + takes.astype(jnp.int32)
    if cores:
        other = 1 - lax.axis_index("depth")
        pl.semaphore_signal(barrier, inc=1, device_id={"depth": other}, device_id_type=MESH)
        expected = expected + 1

    @pl.when(sends)
    def _():
        pl.semaphore_signal(barrier, inc=1, device_id={"tile": outward}, device_id_type=MESH)

    @pl.when(takes)
    def _():
        pl.semaphore_signal(barrier, inc=1, device_id={"tile": inward}, device_id_type=MESH)

    pl.semaphore_wait(barrier, expected)


def remote(src, dst, sems, slot, target):
    return pltpu.make_async_remote_copy(
        src_ref=src, dst_ref=dst, send_sem=sems.at[0, slot], recv_sem=sems.at[1, slot],
        device_id=target, device_id_type=MESH,
    )


def spot(pos_ref, batch, slot, blocks, wide):
    row, column = pos_ref[0, batch, slot, 0], pos_ref[0, batch, slot, 1]
    block = jnp.minimum(lax.shift_right_logical(column, 7), blocks - wide - 1)
    return row, block, column - block * LANES


def main_kernel(
    pos_ref, count_ref, object_ref, meas_ref, probe_ref, prop_ref, dft_ref, dft_t_ref,
    own_ref, recv_ref,
    mine, near, far, ext, send_win, keep_win, recv_win, other, meas, prop, prop_t,
    near_sem, far_sem, win_sem, patch_sem, meas_sem,
):
    odd, partner, outward, inward, sends, takes = route()
    section = lax.axis_index("depth")
    core = {"depth": 1 - section}
    blocks, _, rows, _ = mine.shape
    margin = near.shape[2]
    per = blocks // CHUNKS
    slots, side = own_ref.shape[0], own_ref.shape[2]
    wide = side // LANES
    for block in range(blocks):
        for part in range(2):
            values = object_ref[pl.ds(2 * block + part, rows, stride=2 * blocks), :]
            mine[block, part] = values.astype(bf16)
            ext[block, part, pl.ds(margin, rows), :] = values.astype(bf16).astype(f32)
    greet(True)

    def near_copy(q):
        span = pl.ds(q * per, per)
        return remote(mine.at[span], near.at[span], near_sem, q, {"tile": partner})

    def far_copy(q):
        span = pl.ds(q * per, per)
        return remote(near.at[span], far.at[span], far_sem, q, {"tile": outward})

    def loop(count, body):
        def step(i, carry):
            body(i)
            return carry

        lax.fori_loop(0, count, step, 0)

    loop(CHUNKS, lambda q: near_copy(q).start())
    meas_copy = pltpu.make_async_copy(meas_ref.at[0, section], meas, meas_sem)
    meas_copy.start()

    real, imag = prop_ref[0].astype(f32), prop_ref[1].astype(f32)
    real_t, imag_t = real.T, imag.T
    for ref, re, up, down in ((prop, real, -imag, imag), (prop_t, real_t, imag_t, -imag_t)):
        ref[:side, :side] = re.astype(bf16)
        ref[:side, side:] = up.astype(bf16)
        ref[side:, :side] = down.astype(bf16)
        ref[side:, side:] = re.astype(bf16)

    near_row = pl.multiple_of((1 - odd) * (margin + rows), 8)
    far_row = pl.multiple_of(odd * (margin + rows), 8)

    def fill(q, source, row):
        span = pl.ds(q * per, per)
        ext[span, :, pl.ds(row, source.shape[2]), :] = source[span].astype(f32)

    def pass_on(q):
        near_copy(q).wait_recv()

        @pl.when(sends)
        def _():
            far_copy(q).start()

        fill(q, near, near_row)

    loop(CHUNKS, pass_on)

    def take(q):
        @pl.when(takes)
        def _():
            far_copy(q).wait_recv()
            fill(q, far, far_row)

        @pl.when(jnp.logical_not(takes))
        def _():
            span = pl.ds(q * per, per)
            ext[span, :, pl.ds(far_row, margin), :] = jnp.zeros((per, 2, margin, LANES), f32)

    loop(CHUNKS, take)

    lane = lax.broadcasted_iota(jnp.int32, (side, LANES), 1)

    def cut(out_ref, batch, slot):
        row, block, shift = spot(pos_ref, batch, slot, blocks, wide)
        turn = lax.rem(LANES - shift, LANES)
        inside = lane < LANES - shift
        for part in range(2):
            pieces = [
                pltpu.roll(ext[block + k, part, pl.ds(row, side), :], turn, axis=1)
                for k in range(wide + 1)
            ]
            for k in range(wide):
                out_ref[slot, part, :, k * LANES : (k + 1) * LANES] = jnp.where(
                    inside, pieces[k], pieces[k + 1]
                ).astype(bf16)

    def window_copy(slot):
        return remote(send_win.at[slot], recv_win.at[slot], win_sem, slot, core)

    def patch_copy(slot):
        return remote(other.at[slot], recv_ref.at[slot], patch_sem, slot, core)

    def cut_send(slot):
        cut(send_win, 1 - section, slot)

        @pl.when(slot > 0)
        def _():
            window_copy(slot - 1).start()

    loop(slots, cut_send)

    def cut_keep(slot):
        cut(keep_win, section, slot)

        @pl.when(slot == 0)
        def _():
            window_copy(slots - 1).start()

    loop(slots, cut_keep)
    meas_copy.wait()

    def rounded(whole):
        return whole[:, :side].astype(bf16), whole[:, side:].astype(bf16)

    def times(a, b):
        a, b = [x.astype(f32) for x in a], [x.astype(f32) for x in b]
        return a[0] * b[0] - a[1] * b[1], a[0] * b[1] + a[1] * b[0]

    def conj_times(a, b):
        a, b = [x.astype(f32) for x in a], [x.astype(f32) for x in b]
        return a[0] * b[0] + a[1] * b[1], a[0] * b[1] - a[1] * b[0]

    first = section == 0

    def left_half(left, pair):
        stacked = jnp.concatenate([pair[0].astype(bf16), pair[1].astype(bf16)], axis=0)
        half = jnp.dot(left[...], stacked, preferred_element_type=f32).astype(bf16)
        return jnp.concatenate([half[:side], half[side:]], axis=1)

    def right_half(right, across):
        return jnp.dot(across, right[...], preferred_element_type=f32)

    def slice_window(slot, number):
        return [
            jnp.where(first, keep_win[slot, part], recv_win[slot, part])
            if number == 0
            else jnp.where(first, recv_win[slot, part], keep_win[slot, part])
            for part in range(2)
        ]

    def wave(slot):
        window_copy(slot).wait_recv()
        live = (slot < count_ref[0, section]).astype(f32)
        psi0 = (probe_ref[0], probe_ref[1])
        across = left_half(prop, times(psi0, slice_window(slot, 0)))
        yield
        psi1 = rounded(right_half(prop_t, across))
        yield
        across = left_half(dft_ref, times(psi1, slice_window(slot, 1)))
        yield
        whole = right_half(dft_t_ref, across)
        re, im = whole[:, :side], whole[:, side:]
        misfit = live * (re * re + im * im - meas[slot])
        yield
        across = left_half(dft_t_ref, (misfit * re, misfit * im))
        yield
        g1 = rounded(right_half(dft_ref, across))
        yield
        across = left_half(prop_t, conj_times(slice_window(slot, 1), g1))
        patch1 = conj_times(psi1, g1)
        yield
        g0 = rounded(right_half(prop, across))
        patch0 = conj_times(psi0, g0)
        for part in range(2):
            a, b = patch0[part].astype(bf16), patch1[part].astype(bf16)
            own_ref[slot, part] = jnp.where(first, a, b)
            other[slot, part] = jnp.where(first, b, a)
        if slot > 0:
            patch_copy(slot - 1).start()

    running = [wave(slot) for slot in range(slots)]
    while running:
        running = [chain for chain in running if next(chain, True) is None]

    def settle(q):
        near_copy(q).wait_send()

        @pl.when(sends)
        def _():
            far_copy(q).wait_send()

    loop(CHUNKS, settle)
    loop(slots, lambda slot: window_copy(slot).wait_send())
    patch_copy(slots - 1).start()
    loop(slots, lambda slot: patch_copy(slot).wait())


def add_kernel(pos_ref, own_ref, recv_ref, inner_ref, near_ref, far_ref, total):
    odd = route()[0]
    section = lax.axis_index("depth")
    total[...] = jnp.zeros_like(total)
    slots, side = own_ref.shape[0], own_ref.shape[2]
    wide = side // LANES
    lane = lax.broadcasted_iota(jnp.int32, (side, LANES), 1)

    def add(patch_ref, batch):
        def body(slot, carry):
            row, block, shift = spot(pos_ref, batch, slot, total.shape[0], wide)
            turn = lax.rem(shift, LANES)
            inside = lane >= shift
            for part in range(2):
                pieces = [
                    pltpu.roll(
                        patch_ref[slot, part, :, k * LANES : (k + 1) * LANES].astype(f32),
                        turn,
                        axis=1,
                    )
                    for k in range(wide)
                ]
                pieces = [jnp.zeros_like(pieces[0])] + pieces + [jnp.zeros_like(pieces[0])]
                for k in range(wide + 1):
                    total[block + k, part, pl.ds(row, side), :] += jnp.where(
                        inside, pieces[k + 1], pieces[k]
                    )
            return carry

        lax.fori_loop(0, slots, body, 0)

    add(own_ref, section)
    add(recv_ref, 1 - section)
    margin, rows = near_ref.shape[2], inner_ref.shape[2]
    near_row = pl.multiple_of((1 - odd) * (margin + rows), 8)
    far_row = pl.multiple_of(odd * (margin + rows), 8)
    inner_ref[...] = total[:, :, pl.ds(margin, rows), :]
    near_ref[...] = total[:, :, pl.ds(near_row, margin), :].astype(bf16)
    far_ref[...] = total[:, :, pl.ds(far_row, margin), :].astype(bf16)


def home_kernel(inner_ref, near_ref, far_ref, out_ref, passed, joined, arrived, far_sem, near_sem):
    odd, partner, outward, inward, sends, takes = route()
    blocks = inner_ref.shape[0]
    per = blocks // CHUNKS
    greet(False)

    def loop(body):
        def step(i, carry):
            body(i)
            return carry

        lax.fori_loop(0, CHUNKS, step, 0)

    def far_copy(q):
        span = pl.ds(q * per, per)
        return remote(far_ref.at[span], passed.at[span], far_sem, q, {"tile": inward})

    def near_copy(q):
        span = pl.ds(q * per, per)
        return remote(joined.at[span], arrived.at[span], near_sem, q, {"tile": partner})

    @pl.when(takes)
    def _():
        loop(lambda q: far_copy(q).start())

    def join(q):
        span = pl.ds(q * per, per)

        @pl.when(sends)
        def _():
            far_copy(q).wait_recv()
            joined[span] = (near_ref[span].astype(f32) + passed[span].astype(f32)).astype(bf16)

        @pl.when(jnp.logical_not(sends))
        def _():
            joined[span] = near_ref[span]

        near_copy(q).start()

    loop(join)

    rows = inner_ref.shape[2]
    for q in range(CHUNKS):
        near_copy(q).wait_recv()
        for block in range(q * per, (q + 1) * per):
            for part in range(2):
                out_ref[pl.ds(2 * block + part, rows, stride=2 * blocks), :] = inner_ref[
                    block, part
                ] + arrived[block, part].astype(f32)

    def settle(q):
        near_copy(q).wait_send()

        @pl.when(takes)
        def _():
            far_copy(q).wait_send()

    loop(settle)


def local(object_layer_slices, probe_wave, propagator, positions, counts, measured):
    side = probe_wave.shape[0]
    _, rows, _, columns = object_layer_slices.shape
    slots = positions.shape[2]
    margin = side // 2
    sections, tiles = lax.axis_size("depth"), lax.axis_size("tile")
    assert sections == 2 and positions.shape[1] == sections and object_layer_slices.shape[0] == 1
    assert tiles % 2 == 0 and rows == margin
    blocks = columns // LANES
    extent = (blocks, 2, rows + 2 * margin, LANES)
    tile_shape, window_shape = (blocks, 2, margin, LANES), (slots, 2, side, side)
    tile_bf16 = jax.ShapeDtypeStruct(tile_shape, bf16)
    tile_f32 = jax.ShapeDtypeStruct(tile_shape, f32)
    window = jax.ShapeDtypeStruct(window_shape, bf16)

    lines = jax.ShapeDtypeStruct((rows * blocks * 2, LANES), f32)
    view = object_layer_slices.reshape(rows, 2, blocks, LANES).transpose(0, 2, 1, 3)
    view = view.reshape(lines.shape)
    dft = dft_block(side)
    own, recv = pl.pallas_call(
        main_kernel,
        out_shape=(window, window),
        in_specs=[SMEM, SMEM, VMEM, HBM, VMEM, VMEM, VMEM, VMEM],
        out_specs=(VMEM, VMEM),
        scratch_shapes=[pltpu.VMEM(tile_shape, bf16)] * 3
        + [pltpu.VMEM(extent, f32)]
        + [pltpu.VMEM(window_shape, bf16)] * 4
        + [pltpu.VMEM((slots, side, side), f32)]
        + [pltpu.VMEM((2 * side, 2 * side), bf16)] * 2
        + [pltpu.SemaphoreType.DMA((2, CHUNKS))] * 2
        + [pltpu.SemaphoreType.DMA((2, slots))] * 2
        + [pltpu.SemaphoreType.DMA],
        compiler_params=pltpu.CompilerParams(
            collective_id=0, has_side_effects=True, vmem_limit_bytes=44 << 20
        ),
        name="waves",
    )(
        positions, counts, view, measured, probe_wave.transpose(1, 0, 2),
        propagator.transpose(1, 0, 2), jnp.asarray(dft), jnp.asarray(np.ascontiguousarray(dft.T)),
    )
    inner, near, far = pl.pallas_call(
        add_kernel,
        out_shape=(tile_f32, tile_bf16, tile_bf16),
        in_specs=[SMEM, VMEM, VMEM],
        out_specs=(VMEM, VMEM, VMEM),
        scratch_shapes=[pltpu.VMEM(extent, f32)],
        compiler_params=pltpu.CompilerParams(vmem_limit_bytes=24 << 20),
        name="add",
    )(positions, own, recv)
    total = pl.pallas_call(
        home_kernel,
        out_shape=lines,
        in_specs=[VMEM] * 3,
        out_specs=VMEM,
        scratch_shapes=[pltpu.VMEM(tile_shape, bf16)] * 3
        + [pltpu.SemaphoreType.DMA((2, CHUNKS))] * 2,
        compiler_params=pltpu.CompilerParams(
            collective_id=1, has_side_effects=True, vmem_limit_bytes=20 << 20
        ),
        name="home",
    )(inner, near, far)
    total = total.reshape(rows, blocks, 2, LANES).transpose(0, 2, 1, 3)
    return total.reshape(1, rows, 2, columns)


def solution(mesh):
    placed = (
        P("depth", "tile", None, None),
        P(),
        P(),
        P("tile", None, None, None),
        P("tile", None),
        P("tile", None, None, None, None),
    )
    return jax.shard_map(
        local, mesh=mesh, in_specs=placed, out_specs=P("depth", "tile", None, None), check_vma=False
    )
```

```python
import math

import jax
import jax.numpy as jnp
import numpy as np
from jax import lax
from jax.experimental import pallas as pl
from jax.experimental.pallas import tpu as pltpu
from jax.sharding import PartitionSpec as P

LANES = 128
CHUNKS = 16
MESH = pl.DeviceIdType.MESH
VMEM = pl.BlockSpec(memory_space=pltpu.VMEM)
SMEM = pl.BlockSpec(memory_space=pltpu.SMEM)
HBM = pl.BlockSpec(memory_space=pltpu.HBM)
f32, bf16 = jnp.float32, jnp.bfloat16


def dft_planes(side):
    index = np.arange(side)
    angles = (index[:, None] * index[None, :] % side) * (2.0 * math.pi / side)
    factor = 1.0 / math.sqrt(side)
    planes = np.stack([np.cos(angles) * factor, -np.sin(angles) * factor])
    return planes.astype(np.float32).astype(bf16)


def route():
    tile, tiles = lax.axis_index("tile"), lax.axis_size("tile")
    odd = lax.rem(tile, 2)
    outward = tile + 2 - 4 * odd
    inward = tile - 2 + 4 * odd
    sends = (outward >= 0) & (outward < tiles)
    takes = (inward >= 0) & (inward < tiles)
    return odd, tile + 1 - 2 * odd, outward, inward, sends, takes


def greet(cores):
    odd, partner, outward, inward, sends, takes = route()
    barrier = pltpu.get_barrier_semaphore()
    pl.semaphore_signal(barrier, inc=1, device_id={"tile": partner}, device_id_type=MESH)
    expected = 1 + sends.astype(jnp.int32) + takes.astype(jnp.int32)
    if cores:
        other = 1 - lax.axis_index("depth")
        pl.semaphore_signal(barrier, inc=1, device_id={"depth": other}, device_id_type=MESH)
        expected = expected + 1

    @pl.when(sends)
    def _():
        pl.semaphore_signal(barrier, inc=1, device_id={"tile": outward}, device_id_type=MESH)

    @pl.when(takes)
    def _():
        pl.semaphore_signal(barrier, inc=1, device_id={"tile": inward}, device_id_type=MESH)

    pl.semaphore_wait(barrier, expected)


def remote(src, dst, sems, slot, target):
    return pltpu.make_async_remote_copy(
        src_ref=src, dst_ref=dst, send_sem=sems.at[0, slot], recv_sem=sems.at[1, slot],
        device_id=target, device_id_type=MESH,
    )


def spot(pos_ref, batch, slot, blocks, wide):
    row, column = pos_ref[0, batch, slot, 0], pos_ref[0, batch, slot, 1]
    block = jnp.minimum(lax.shift_right_logical(column, 7), blocks - wide - 1)
    return row, block, column - block * LANES


def main_kernel(
    pos_ref, count_ref, object_ref, meas_ref, probe_ref, prop_ref, fourier_ref,
    own_ref, recv_ref,
    lines, dft_ref, dft_t_ref, mine, near, far, ext, send_win, keep_win, recv_win, other, meas, prop, prop_t,
    near_sem, far_sem, win_sem, patch_sem, load_sem,
):
    odd, partner, outward, inward, sends, takes = route()
    section = lax.axis_index("depth")
    core = {"depth": 1 - section}
    blocks, _, rows, _ = mine.shape
    margin = near.shape[2]
    per = blocks // CHUNKS
    slots, side = own_ref.shape[0], own_ref.shape[2]
    wide = side // LANES
    object_copy = pltpu.make_async_copy(object_ref, lines, load_sem.at[0])
    object_copy.start()
    meas_copy = pltpu.make_async_copy(meas_ref.at[0, section], meas, load_sem.at[1])
    greet(True)

    def near_copy(q):
        span = pl.ds(q * per, per)
        return remote(mine.at[span], near.at[span], near_sem, q, {"tile": partner})

    def far_copy(q):
        span = pl.ds(q * per, per)
        return remote(near.at[span], far.at[span], far_sem, q, {"tile": outward})

    def loop(count, body):
        def step(i, carry):
            body(i)
            return carry

        lax.fori_loop(0, count, step, 0)

    object_copy.wait()
    for q in range(CHUNKS):
        for block in range(q * per, (q + 1) * per):
            for part in range(2):
                values = lines[pl.ds(2 * block + part, rows, stride=2 * blocks), :].astype(bf16)
                mine[block, part] = values
                ext[block, part, pl.ds(margin, rows), :] = values.astype(f32)
        if q > 0:
            near_copy(q - 1).start()
    near_copy(CHUNKS - 1).start()
    meas_copy.start()

    def expand(source, block, block_t):
        real, imag = source[0].astype(f32), source[1].astype(f32)
        real_t, imag_t = real.T, imag.T
        for ref, same, up, down in (
            (block, real, -imag, imag), (block_t, real_t, imag_t, -imag_t)
        ):
            ref[:side, :side] = same.astype(bf16)
            ref[:side, side:] = up.astype(bf16)
            ref[side:, :side] = down.astype(bf16)
            ref[side:, side:] = same.astype(bf16)

    expand(prop_ref, prop, prop_t)
    expand(fourier_ref, dft_ref, dft_t_ref)

    near_row = pl.multiple_of((1 - odd) * (margin + rows), 8)
    far_row = pl.multiple_of(odd * (margin + rows), 8)

    def fill(q, source, row):
        span = pl.ds(q * per, per)
        ext[span, :, pl.ds(row, source.shape[2]), :] = source[span].astype(f32)

    def pass_on(q):
        near_copy(q).wait_recv()

        @pl.when(sends)
        def _():
            far_copy(q).start()

        fill(q, near, near_row)

    loop(CHUNKS, pass_on)

    def take(q):
        @pl.when(takes)
        def _():
            far_copy(q).wait_recv()
            fill(q, far, far_row)

        @pl.when(jnp.logical_not(takes))
        def _():
            span = pl.ds(q * per, per)
            ext[span, :, pl.ds(far_row, margin), :] = jnp.zeros((per, 2, margin, LANES), f32)

    loop(CHUNKS, take)

    lane = lax.broadcasted_iota(jnp.int32, (side, LANES), 1)

    def cut(out_ref, batch, slot):
        row, block, shift = spot(pos_ref, batch, slot, blocks, wide)
        turn = lax.rem(LANES - shift, LANES)
        inside = lane < LANES - shift
        for part in range(2):
            pieces = [
                pltpu.roll(ext[block + k, part, pl.ds(row, side), :], turn, axis=1)
                for k in range(wide + 1)
            ]
            for k in range(wide):
                out_ref[slot, part, :, k * LANES : (k + 1) * LANES] = jnp.where(
                    inside, pieces[k], pieces[k + 1]
                ).astype(bf16)

    def window_copy(slot):
        return remote(send_win.at[slot], recv_win.at[slot], win_sem, slot, core)

    def patch_copy(slot):
        return remote(other.at[slot], recv_ref.at[slot], patch_sem, slot, core)

    def cut_send(slot):
        cut(send_win, 1 - section, slot)

        @pl.when(slot > 0)
        def _():
            window_copy(slot - 1).start()

    loop(slots, cut_send)

    def cut_keep(slot):
        cut(keep_win, section, slot)

        @pl.when(slot == 0)
        def _():
            window_copy(slots - 1).start()

    loop(slots, cut_keep)
    meas_copy.wait()

    def rounded(whole):
        return whole[:, :side].astype(bf16), whole[:, side:].astype(bf16)

    def times(a, b):
        a, b = [x.astype(f32) for x in a], [x.astype(f32) for x in b]
        return a[0] * b[0] - a[1] * b[1], a[0] * b[1] + a[1] * b[0]

    def conj_times(a, b):
        a, b = [x.astype(f32) for x in a], [x.astype(f32) for x in b]
        return a[0] * b[0] + a[1] * b[1], a[0] * b[1] - a[1] * b[0]

    first = section == 0

    def left_half(left, pair):
        stacked = jnp.concatenate([pair[0].astype(bf16), pair[1].astype(bf16)], axis=0)
        half = jnp.dot(left[...], stacked, preferred_element_type=f32).astype(bf16)
        return jnp.concatenate([half[:side], half[side:]], axis=1)

    def right_half(right, across):
        return jnp.dot(across, right[...], preferred_element_type=f32)

    def slice_window(slot, number):
        return [
            jnp.where(first, keep_win[slot, part], recv_win[slot, part])
            if number == 0
            else jnp.where(first, recv_win[slot, part], keep_win[slot, part])
            for part in range(2)
        ]

    def wave(slot):
        window_copy(slot).wait_recv()
        live = (slot < count_ref[0, section]).astype(f32)
        psi0 = (probe_ref[0], probe_ref[1])
        across = left_half(prop, times(psi0, slice_window(slot, 0)))
        yield
        psi1 = rounded(right_half(prop_t, across))
        yield
        across = left_half(dft_ref, times(psi1, slice_window(slot, 1)))
        yield
        whole = right_half(dft_t_ref, across)
        re, im = whole[:, :side], whole[:, side:]
        misfit = live * (re * re + im * im - meas[slot])
        yield
        across = left_half(dft_t_ref, (misfit * re, misfit * im))
        yield
        g1 = rounded(right_half(dft_ref, across))
        yield
        across = left_half(prop_t, conj_times(slice_window(slot, 1), g1))
        patch1 = conj_times(psi1, g1)
        yield
        g0 = rounded(right_half(prop, across))
        patch0 = conj_times(psi0, g0)
        for part in range(2):
            a, b = patch0[part].astype(bf16), patch1[part].astype(bf16)
            own_ref[slot, part] = jnp.where(first, a, b)
            other[slot, part] = jnp.where(first, b, a)
        if slot > 0:
            patch_copy(slot - 1).start()

    running = [wave(slot) for slot in range(slots)]
    while running:
        running = [chain for chain in running if next(chain, True) is None]

    def settle(q):
        near_copy(q).wait_send()

        @pl.when(sends)
        def _():
            far_copy(q).wait_send()

    loop(CHUNKS, settle)
    loop(slots, lambda slot: window_copy(slot).wait_send())
    patch_copy(slots - 1).start()
    loop(slots, lambda slot: patch_copy(slot).wait())


def add_kernel(pos_ref, own_ref, recv_ref, inner_ref, near_ref, far_ref, total):
    odd = route()[0]
    section = lax.axis_index("depth")
    total[...] = jnp.zeros_like(total)
    slots, side = own_ref.shape[0], own_ref.shape[2]
    wide = side // LANES
    lane = lax.broadcasted_iota(jnp.int32, (side, LANES), 1)

    def add(patch_ref, batch):
        def body(slot, carry):
            row, block, shift = spot(pos_ref, batch, slot, total.shape[0], wide)
            turn = lax.rem(shift, LANES)
            inside = lane >= shift
            for part in range(2):
                pieces = [
                    pltpu.roll(
                        patch_ref[slot, part, :, k * LANES : (k + 1) * LANES].astype(f32),
                        turn,
                        axis=1,
                    )
                    for k in range(wide)
                ]
                pieces = [jnp.zeros_like(pieces[0])] + pieces + [jnp.zeros_like(pieces[0])]
                for k in range(wide + 1):
                    total[block + k, part, pl.ds(row, side), :] += jnp.where(
                        inside, pieces[k + 1], pieces[k]
                    )
            return carry

        lax.fori_loop(0, slots, body, 0)

    add(own_ref, section)
    add(recv_ref, 1 - section)
    margin, rows = near_ref.shape[2], inner_ref.shape[2]
    near_row = pl.multiple_of((1 - odd) * (margin + rows), 8)
    far_row = pl.multiple_of(odd * (margin + rows), 8)
    inner_ref[...] = total[:, :, pl.ds(margin, rows), :]
    near_ref[...] = total[:, :, pl.ds(near_row, margin), :].astype(bf16)
    far_ref[...] = total[:, :, pl.ds(far_row, margin), :].astype(bf16)


def home_kernel(inner_ref, near_ref, far_ref, out_ref, passed, joined, arrived, far_sem, near_sem):
    odd, partner, outward, inward, sends, takes = route()
    blocks = inner_ref.shape[0]
    per = blocks // CHUNKS
    greet(False)

    def loop(body):
        def step(i, carry):
            body(i)
            return carry

        lax.fori_loop(0, CHUNKS, step, 0)

    def far_copy(q):
        span = pl.ds(q * per, per)
        return remote(far_ref.at[span], passed.at[span], far_sem, q, {"tile": inward})

    def near_copy(q):
        span = pl.ds(q * per, per)
        return remote(joined.at[span], arrived.at[span], near_sem, q, {"tile": partner})

    @pl.when(takes)
    def _():
        loop(lambda q: far_copy(q).start())

    def join(q):
        span = pl.ds(q * per, per)

        @pl.when(sends)
        def _():
            far_copy(q).wait_recv()
            joined[span] = (near_ref[span].astype(f32) + passed[span].astype(f32)).astype(bf16)

        @pl.when(jnp.logical_not(sends))
        def _():
            joined[span] = near_ref[span]

        near_copy(q).start()

    loop(join)

    rows = inner_ref.shape[2]
    for q in range(CHUNKS):
        near_copy(q).wait_recv()
        for block in range(q * per, (q + 1) * per):
            for part in range(2):
                out_ref[pl.ds(2 * block + part, rows, stride=2 * blocks), :] = inner_ref[
                    block, part
                ] + arrived[block, part].astype(f32)

    def settle(q):
        near_copy(q).wait_send()

        @pl.when(takes)
        def _():
            far_copy(q).wait_send()

    loop(settle)


def local(object_layer_slices, probe_wave, propagator, positions, counts, measured):
    side = probe_wave.shape[0]
    _, rows, _, columns = object_layer_slices.shape
    slots = positions.shape[2]
    margin = side // 2
    sections, tiles = lax.axis_size("depth"), lax.axis_size("tile")
    assert sections == 2 and positions.shape[1] == sections and object_layer_slices.shape[0] == 1
    assert tiles % 2 == 0 and rows == margin
    blocks = columns // LANES
    extent = (blocks, 2, rows + 2 * margin, LANES)
    tile_shape, window_shape = (blocks, 2, margin, LANES), (slots, 2, side, side)
    tile_bf16 = jax.ShapeDtypeStruct(tile_shape, bf16)
    tile_f32 = jax.ShapeDtypeStruct(tile_shape, f32)
    window = jax.ShapeDtypeStruct(window_shape, bf16)

    lines = jax.ShapeDtypeStruct((rows * blocks * 2, LANES), f32)
    view = object_layer_slices.reshape(rows, 2, blocks, LANES).transpose(0, 2, 1, 3)
    view = view.reshape(lines.shape)
    own, recv = pl.pallas_call(
        main_kernel,
        out_shape=(window, window),
        in_specs=[SMEM, SMEM, HBM, HBM, VMEM, VMEM, VMEM],
        out_specs=(VMEM, VMEM),
        scratch_shapes=[pltpu.VMEM(lines.shape, f32)]
        + [pltpu.VMEM((2 * side, 2 * side), bf16)] * 2
        + [pltpu.VMEM(tile_shape, bf16)] * 3
        + [pltpu.VMEM(extent, f32)]
        + [pltpu.VMEM(window_shape, bf16)] * 4
        + [pltpu.VMEM((slots, side, side), f32)]
        + [pltpu.VMEM((2 * side, 2 * side), bf16)] * 2
        + [pltpu.SemaphoreType.DMA((2, CHUNKS))] * 2
        + [pltpu.SemaphoreType.DMA((2, slots))] * 2
        + [pltpu.SemaphoreType.DMA((2,))],
        compiler_params=pltpu.CompilerParams(
            collective_id=0, has_side_effects=True, vmem_limit_bytes=49 << 20
        ),
        name="waves",
    )(
        positions, counts, view, measured, probe_wave.transpose(1, 0, 2),
        propagator.transpose(1, 0, 2), jnp.asarray(dft_planes(side)),
    )
    inner, near, far = pl.pallas_call(
        add_kernel,
        out_shape=(tile_f32, tile_bf16, tile_bf16),
        in_specs=[SMEM, VMEM, VMEM],
        out_specs=(VMEM, VMEM, VMEM),
        scratch_shapes=[pltpu.VMEM(extent, f32)],
        compiler_params=pltpu.CompilerParams(vmem_limit_bytes=24 << 20),
        name="add",
    )(positions, own, recv)
    total = pl.pallas_call(
        home_kernel,
        out_shape=lines,
        in_specs=[VMEM] * 3,
        out_specs=VMEM,
        scratch_shapes=[pltpu.VMEM(tile_shape, bf16)] * 3
        + [pltpu.SemaphoreType.DMA((2, CHUNKS))] * 2,
        compiler_params=pltpu.CompilerParams(
            collective_id=1, has_side_effects=True, vmem_limit_bytes=20 << 20
        ),
        name="home",
    )(inner, near, far)
    total = total.reshape(rows, blocks, 2, LANES).transpose(0, 2, 1, 3)
    return total.reshape(1, rows, 2, columns)


def solution(mesh):
    placed = (
        P("depth", "tile", None, None),
        P(),
        P(),
        P("tile", None, None, None),
        P("tile", None),
        P("tile", None, None, None, None),
    )
    return jax.shard_map(
        local, mesh=mesh, in_specs=placed, out_specs=P("depth", "tile", None, None), check_vma=False
    )
```
